256 devices in a mesh: ops: 8 (over x, core), sec: 32 (over z, y).
Axes of the slice: x: 4, y: 4, z: 8, core: 2. Of those that a mesh axis runs over, the one named last changes fastest.
Arguments:
- wavefunction: float32 [256, 2, 128, 128], P('sec'), may hold values from -6 to 6
- left_blocks: float32 [64, 256, 128, 128], P('ops', 'sec'), may hold values from -0.5 to 0.5
- right_blocks: float32 [64, 256, 128, 128], P('ops', 'sec'), may hold values from -0.0625 to 0.0625
- target_owner: int32 [8, 32, 8, 8, 1], P('ops'), may hold values from 0 to 31; in each aligned block of 64 rows (0 to 63, 64 to 127, ..., all dimensions but the last counted through in order) at most 3 rows name the same one
- target_local: int32 [8, 32, 8, 8], P('ops'), may hold values from 0 to 7
Outputs:
- sigma: float32 [256, 2, 128, 128], P('sec', None, 'ops')
The draws below stay inside these ranges and needn't reach their ends.
Inputs may be any that keep to these rules, and one draw needn't show every extreme that they name: `target_owner`: among the 64 pairs [o, d, :, :, 0] of one device, at most 3 name the same owner, and some device's pairs name one owner exactly 3 times.
All inputs are finite; a program needn't handle non-finite values.
Results may differ from the reference program's by a relative error of at most 0.00013.
Values sent between devices are 32-bit elements; how exact they have to be, the bound alone decides.
A program may use at most 192 MiB of HBM per device.

```python
import math
import jax
import jax.numpy as jnp
import numpy as np
from jax import lax

M = 128
NVEC = 2
TERM_DEV = 8
SEC_DEV = 8
TERMS = 64
NSEC = 256
CAP = 3
N_OPS = 8
N_SEC = 32


def place_ends(result, rng, low, largest):
    index_at = [jax.random.randint(jax.random.fold_in(rng, axis), (), 0, length) for axis, length in enumerate(result.shape)]
    main_axis = result.shape.index(max(result.shape))
    next_to = index_at[:main_axis] + [(index_at[main_axis] + 1) % result.shape[main_axis]] + index_at[main_axis + 1:]
    return result.at[tuple(index_at)].set(low).at[tuple(next_to)].set(largest)


def steps_of(key, shape, split, least, top_value):
    def one(position, shards_of):
        draws = jax.random.uniform(jax.random.fold_in(jax.random.fold_in(key, 6), position), (shards_of,), jnp.float32, least / len(split), top_value / len(split))
        return jnp.repeat(jnp.exp(draws), shape[position] // shards_of).reshape((-1,) + (1,) * (len(shape) - position - 1))

    factor_of = one(*split[0])
    for cut in split[1:]:
        factor_of = factor_of * one(*cut)
    return factor_of


def assign_block(key, own, number, rows, count, top, reach, lean):
    order = jax.random.permutation(key, count)
    heavy_load, common = shares(count, rows * top, reach, lean, True), shares(count, rows * top, reach, lean, False)
    places = jnp.arange(count)

    def named(tallies, rotation):
        used = int((tallies > 0).sum())
        fixed = max(1, used // 4)
        moved = fixed + (places - fixed + rotation * (used - fixed)) % max(1, count - fixed)
        return jnp.zeros((count,), jnp.int32).at[order[jnp.where(places < fixed, places, moved)]].set(jnp.asarray(tallies, jnp.int32))

    tallies = jnp.where(number % 4 == 0, named(heavy_load, number // 4), named(common, number - number // 4 - 1))
    mixed = jax.random.permutation(jax.random.fold_in(own, 3), count)
    source_of, sink = mixed[0:count // 2 * 2:2], mixed[1:count // 2 * 2:2]
    slack = jnp.minimum(tallies[source_of] - 1, reach - tallies[sink]) // 2
    slack = jnp.where((source_of == order[0]) | (sink == order[0]) | (tallies[sink] == 0), 0, jnp.maximum(slack, 0))
    moved = jax.random.randint(jax.random.fold_in(own, 4), (count // 2,), 0, 1 << 20) % (slack + 1)
    tallies = tallies.at[source_of].add(-moved).at[sink].add(moved)
    members = jnp.searchsorted(jnp.cumsum(tallies), jnp.arange(rows * top), side="right").astype(jnp.int32)
    table = members.reshape(top, rows).T
    table = table[jax.random.permutation(jax.random.fold_in(own, 1), rows)]
    rotation = jax.random.randint(jax.random.fold_in(own, 2), (rows, 1), 0, top)
    return jnp.take_along_axis(table, (jnp.arange(top)[None, :] + rotation) % top, axis=1)


def shares(amount, total, most, lean, full):
    portions = [(1 << 20) // math.isqrt(standing ** lean) + 1 for standing in range(1, amount + 1)]
    largest = most if full else min(most, max(-(-total // amount), total * portions[0] // sum(portions)))
    least = 1 if total - largest >= amount - 1 else 0
    given, surplus = [largest] + [least] * (amount - 1), total - largest - least * (amount - 1)
    while surplus > 0:
        free = [i for i in range(1, amount) if given[i] < largest] or [i for i in range(1, amount) if given[i] < most]
        pool, budget = sum([portions[i] for i in free]), surplus
        for i in free:
            addition = min(most - given[i], max(1, budget * portions[i] // pool), surplus)
            given[i] = given[i] + addition
            surplus = surplus - addition
    return np.array(given)


def centred(key, extent, width, reach, shards=(), kind=jnp.bfloat16):
    level = steps_of(key, extent, shards, -0.22, 0.18) if shards else 1.0
    entries = jax.random.normal(key, extent, jnp.float32) * width * level
    return jnp.minimum(jnp.maximum(entries, -reach), reach).astype(kind)


def setup_inputs(seed: int = 0) -> dict:
    keys = jax.random.split(jax.random.key(seed), 6)
    wavefunction = centred(keys[0], (NSEC, NVEC, M, M), 1.0, 6.0, ((0, 32),), jnp.float32)
    left_blocks = centred(keys[1], (TERMS, NSEC, M, M), M ** -0.5, 0.5, ((0, 8), (1, 32)), jnp.float32)
    right_blocks = centred(keys[2], (TERMS, NSEC, M, M), (M * TERMS) ** -0.5, 0.0625, ((0, 8), (1, 32)), jnp.float32)
    target_owner_keys = jax.random.split(jax.random.fold_in(keys[3], 1), N_OPS * N_SEC * TERM_DEV * SEC_DEV // (TERM_DEV * SEC_DEV))
    target_owner_turns = jax.random.permutation(jax.random.fold_in(keys[3], 3), N_OPS * N_SEC * TERM_DEV * SEC_DEV // (TERM_DEV * SEC_DEV))
    target_owner = jax.vmap(lambda own, number: assign_block(jax.random.fold_in(keys[3], 2), own, number, TERM_DEV * SEC_DEV, N_SEC, 1, CAP, 2))(target_owner_keys, target_owner_turns).reshape((N_OPS, N_SEC, TERM_DEV, SEC_DEV, 1))
    target_local = place_ends(jax.random.randint(keys[4], (N_OPS, N_SEC, TERM_DEV, SEC_DEV), 0, SEC_DEV), jax.random.fold_in(keys[4], 1), 0, SEC_DEV - 1).astype(jnp.int32)
    return {"wavefunction": wavefunction, "left_blocks": left_blocks, "right_blocks": right_blocks, "target_owner": target_owner, "target_local": target_local}


def reference(wavefunction, left_blocks, right_blocks, target_owner, target_local):
    owner_table = jnp.transpose(target_owner[..., 0], (0, 2, 1, 3)).reshape(TERMS, NSEC)
    local_table = jnp.transpose(target_local, (0, 2, 1, 3)).reshape(TERMS, NSEC)
    targets = (owner_table * SEC_DEV + local_table).astype(jnp.int32)
    exact_mode = lax.Precision.HIGHEST

    def add_term(running, per_term):
        left_block, right_block, term_targets = per_term
        half_applied = jnp.einsum('svbe,sde->svbd', wavefunction.astype(jnp.float32), right_block.astype(jnp.float32), precision=exact_mode)
        contrib = jnp.einsum('sab,svbd->svad', left_block.astype(jnp.float32), half_applied, precision=exact_mode)
        return running + jax.ops.segment_sum(contrib, term_targets, num_segments=NSEC), None

    initial = jnp.zeros((NSEC, NVEC, M, M), jnp.float32)
    sigma, unused = lax.scan(add_term, initial, (left_blocks, right_blocks, targets))
    return sigma
```

```python
import jax
import jax.numpy as jnp
from jax import lax
from jax.sharding import PartitionSpec as P


def shards(wavefunction, left_blocks, right_blocks, target_owner, target_local):
    sec_count = lax.axis_size("sec")
    ops_count = lax.axis_size("ops")
    term_local, sector_local, states = left_blocks.shape[:3]
    vectors = wavefunction.shape[1]
    pair_count = term_local * sector_local
    rows = states // ops_count
    me = lax.axis_index("sec")
    owner = lax.dynamic_index_in_dim(target_owner[0, :, :, :, 0], me, 0, keepdims=False)
    local = lax.dynamic_index_in_dim(target_local[0], me, 0, keepdims=False)
    target = (owner * sector_local + local).reshape(pair_count)
    targets = lax.all_gather(target, "ops", axis=0, tiled=True)
    high = lax.Precision.HIGH
    half = jnp.einsum("jvbe,kjde->kjvbd", wavefunction, right_blocks, precision=high)
    contrib = jnp.einsum("kjab,kjvbd->kjvad", left_blocks, half, precision=high)
    split = contrib.reshape(pair_count, vectors, ops_count, rows, states)
    split = split.transpose(2, 0, 1, 3, 4)
    arrived = lax.all_to_all(split, "ops", split_axis=0, concat_axis=0, tiled=True)
    flat = arrived.reshape(ops_count * pair_count, vectors * rows * states)
    total = sec_count * sector_local
    selector = (targets[None, :] == jnp.arange(total, dtype=jnp.int32)[:, None]).astype(jnp.float32)
    dense = jnp.dot(selector, flat, precision=high, preferred_element_type=jnp.float32)
    dense = dense.reshape(total, vectors, rows, states)
    return lax.psum_scatter(dense, "sec", scatter_dimension=0, tiled=True)


def solution(mesh):
    placed = (
        P("sec", None, None, None),
        P("ops", "sec", None, None),
        P("ops", "sec", None, None),
        P("ops", None, None, None, None),
        P("ops", None, None, None),
    )
    return jax.shard_map(
        shards, mesh=mesh, in_specs=placed, out_specs=P("sec", None, "ops", None), check_vma=False
    )
```

```python
import functools
import jax
import jax.numpy as jnp
from jax import lax
from jax.experimental import pallas as pl
from jax.experimental.pallas import tpu as pltpu
from jax.sharding import PartitionSpec as P

MESH = pl.DeviceIdType.MESH
F32, BF16 = jnp.float32, jnp.bfloat16
PAIRS, STATES, SECTORS, GROUPS = 64, 128, 8, 4
PER = PAIRS // GROUPS
TARGETS, NX, NY, NZ = 256, 4, 4, 8


def split(value):
    high = value.astype(BF16)
    return high, (value - high.astype(F32)).astype(BF16)


def dev(x, c, y, z):
    return (x * 2 + c, z * NY + y)


def kernel(tab_ref, psi_hbm, left_hbm, right_hbm, out_ref,
           psi, psic, left, right, send, recv, dense, recv2, send3, recv3, tabs, hot,
           in_sem, tab_s, tab_r, s1_s, s1_r, own_sem, s2_s, s2_r, s3_s, s3_r):
    o, s = lax.axis_index("ops"), lax.axis_index("sec")
    x, c, y, z = o // 2, o % 2, s % NY, s // NY
    own = (o, y * 2 + c)

    def row_peer(v, r):
        return dev(r // 2, r % 2, y, z) if v == 0 else dev(x, r % 2, r // 2, z)

    def dense_peer(v, b):
        return dev(x, c, b, z) if v == 0 else dev(b, c, y, z)

    def home_peer(v, b):
        return dev(x, c, y, b) if v == 0 else dev(y, c, x, b)

    psi_copy = pltpu.make_async_copy(psi_hbm, psi, in_sem.at[2, 0])
    psi_copy.start()

    def block_copies(g):
        rows = pl.ds(g * PER, PER)
        return (
            pltpu.make_async_copy(left_hbm.at[rows], left.at[rows], in_sem.at[0, g]),
            pltpu.make_async_copy(right_hbm.at[rows], right.at[rows], in_sem.at[1, g]),
        )

    for g in range(GROUPS):
        for copy in block_copies(g):
            copy.start()

    barrier = pltpu.get_barrier_semaphore()

    def greet(peer):
        pl.semaphore_signal(barrier, inc=1, device_id=peer, device_id_type=MESH)

    for d in range(1, 8):
        greet(row_peer(0, (own[0] + d) % 8))
        if d != 1:
            r = (own[1] // 2 + d // 2) % NY * 2 + (c + d) % 2
            greet(row_peer(1, r))
        greet(home_peer(0, (z + d) % NZ))

    @pl.when(x != y)
    def _():
        for d in range(NZ):
            greet(home_peer(1, (z + d) % NZ))

    pl.semaphore_wait(barrier, jnp.where(x == y, 20, 20 + NZ))

    def other(v, d):
        return (own[v] // 2 + d // 2) % 4 * 2 + (c + d) % 2

    def tab_copy(v, d):
        r = other(v, d)
        return pltpu.make_async_remote_copy(
            src_ref=tab_ref, dst_ref=tabs.at[v, own[v]],
            send_sem=tab_s.at[v, r], recv_sem=tab_r.at[v, own[v]],
            device_id=row_peer(v, r), device_id_type=MESH)

    def tab_wait(v, d):
        r = other(v, d)
        return pltpu.make_async_remote_copy(
            src_ref=tab_ref, dst_ref=tabs.at[v, r],
            send_sem=tab_s.at[v, r], recv_sem=tab_r.at[v, r],
            device_id=row_peer(v, r), device_id_type=MESH)

    def row_copy(v, h, d, rows):
        r = other(v, d)
        return pltpu.make_async_remote_copy(
            src_ref=send.at[v, h, r, rows], dst_ref=recv.at[v, h, own[v], rows],
            send_sem=s1_s.at[v, h, r], recv_sem=s1_r.at[v, h, own[v]],
            device_id=row_peer(v, r), device_id_type=MESH)

    def row_wait(v, h, d):
        r = other(v, d)
        return pltpu.make_async_remote_copy(
            src_ref=send.at[v, h, r], dst_ref=recv.at[v, h, r],
            send_sem=s1_s.at[v, h, r], recv_sem=s1_r.at[v, h, r],
            device_id=row_peer(v, r), device_id_type=MESH)

    for d in range(1, 8):
        for v in range(2):
            tab_copy(v, d).start()
    for v in range(2):
        tabs[v, own[v]] = tab_ref[...]

    psi_copy.wait()

    @pl.loop(0, SECTORS)
    def _(j):
        high, low = split(psi[j].reshape(2 * STATES, STATES))
        psic[j] = jnp.concatenate([high, high, low], axis=1)

    @pl.loop(0, GROUPS)
    def _(g):
        for copy in block_copies(g):
            copy.wait()

        @pl.loop(0, PER)
        def _(i):
            p = g * PER + i
            high, low = split(right[p])
            half = lax.dot_general(
                psic[p % SECTORS], jnp.concatenate([high, low, high], axis=1),
                (((1,), (1,)), ((), ())), preferred_element_type=F32)
            wide = jnp.concatenate([half[:STATES], half[STATES:]], axis=1)
            high, low = split(wide)
            operand = jnp.concatenate([high, low, high], axis=0)
            high, low = split(left[p])
            product = jnp.dot(
                jnp.concatenate([high, high, low], axis=1), operand, preferred_element_type=F32)
            for q in range(16):
                for v in range(2):
                    send[v, q % 2, q // 2, p] = product[8 * q:8 * q + 8, STATES * v:STATES * (v + 1)]

        for d in range(1, 8):
            for v in range(2):
                row_copy(v, 0, d, pl.ds(g * PER, PER)).start()

    for d in range(1, 8):
        for v in range(2):
            row_copy(v, 1, d, pl.ds(0, PAIRS)).start()

    def own_copy(v, h):
        return pltpu.make_async_copy(send.at[v, h, own[v]], recv.at[v, h, own[v]], own_sem.at[v, h])

    for h in range(2):
        for v in range(2):
            own_copy(v, h).start()

    for v in range(2):
        for d in range(1, 8):
            tab_wait(v, d).wait()
        for q in range(4):
            line = tabs[v, 2 * q][0:1, :] + tabs[v, 2 * q + 1][0:1, :]
            number = lax.broadcasted_iota(jnp.int32, (TARGETS, 128), 0)
            hot[v, :, 128 * q:128 * (q + 1)] = (number == line).astype(F32).astype(BF16)

    def dense_copy(v, h, d):
        b = ((y, x)[v] + d) % 4
        return pltpu.make_async_remote_copy(
            src_ref=dense.at[v, h, pl.ds(b * 512, 512)], dst_ref=recv2.at[v, h, d - 1],
            send_sem=s2_s.at[v, h, d - 1], recv_sem=s2_r.at[v, h, d - 1],
            device_id=dense_peer(v, b), device_id_type=MESH)

    def home_copy(v, h, d):
        b = (z + d) % NZ
        return pltpu.make_async_remote_copy(
            src_ref=send3.at[v, h, b], dst_ref=recv3.at[v, h, d],
            send_sem=s3_s.at[v, h, d], recv_sem=s3_r.at[v, h, d],
            device_id=home_peer(v, b), device_id_type=MESH)

    for h in range(2):
        for v in range(2):
            for d in range(1, 8):
                row_wait(v, h, d).wait_recv()
            own_copy(v, h).wait()
            flat = recv.at[v, h].reshape(8 * PAIRS * 8, 128)

            for i in range(8):
                high, low = split(flat[pl.ds(i, 512, stride=8), :])
                total = jnp.dot(hot[v], jnp.concatenate([high, low], axis=1), preferred_element_type=F32)
                dense[v, h, pl.ds(i, TARGETS, stride=8), :] = total[:, :128] + total[:, 128:]

            for d in range(1, 4):
                dense_copy(v, h, d).start()

        for v in range(2):
            for d in range(1, 4):
                dense_copy(v, h, d).wait_recv()
            mine = dense[v, h, pl.ds((y, x)[v] * 512, 512), :]
            total = mine + recv2[v, h, 0] + recv2[v, h, 1] + recv2[v, h, 2]
            send3[v, h] = total.reshape(NZ, SECTORS * 8, 128)
            for d in range(1, NZ):
                home_copy(v, h, d).start()
            if v == 0:
                recv3[v, h, 0] = send3[v, h, z]
            else:
                @pl.when(x == y)
                def _():
                    recv3[v, h, 0] = send3[v, h, z]

                @pl.when(x != y)
                def _():
                    home_copy(v, h, 0).start()

    for h in range(2):
        for v in range(2):
            for d in range(1, NZ):
                home_copy(v, h, d).wait_recv()
            if v == 1:
                @pl.when(x != y)
                def _():
                    home_copy(v, h, 0).wait_recv()
            total = recv3[v, h, 0]
            for d in range(1, NZ):
                total = total + recv3[v, h, d]
            out_ref[:, v, 8 * h:8 * h + 8, :] = total.reshape(SECTORS, 8, 128)

    for h in range(2):
        for v in range(2):
            for d in range(1, 8):
                row_wait(v, h, d).wait_send()
            for d in range(1, 4):
                dense_copy(v, h, d).wait_send()
            for d in range(1, NZ):
                home_copy(v, h, d).wait_send()

        @pl.when(x != y)
        def _():
            home_copy(1, h, 0).wait_send()


def shards(wavefunction, left_blocks, right_blocks, target_owner, target_local):
    o, s = lax.axis_index("ops"), lax.axis_index("sec")
    owner = lax.dynamic_index_in_dim(target_owner[0, :, :, :, 0], s, 0, keepdims=False)
    local = lax.dynamic_index_in_dim(target_local[0], s, 0, keepdims=False)
    line = (owner % NY * (NZ * SECTORS) + owner // NY * SECTORS + local).reshape(1, PAIRS)
    lanes = jnp.arange(128, dtype=jnp.int32)[None, :]
    table = jnp.where(lanes // PAIRS == o % 2, jnp.concatenate([line, line], axis=1), 0)
    table = jnp.broadcast_to(table, (8, 128))
    left = left_blocks.reshape(PAIRS, STATES, STATES)
    right = right_blocks.reshape(PAIRS, STATES, STATES)
    anywhere = pl.BlockSpec(memory_space=pl.ANY)
    near = pl.BlockSpec(memory_space=pltpu.VMEM)
    dma = pltpu.SemaphoreType.DMA
    return pl.pallas_call(
        kernel,
        out_shape=jax.ShapeDtypeStruct((SECTORS, 2, 16, STATES), F32),
        in_specs=[near, anywhere, anywhere, anywhere],
        out_specs=near,
        scratch_shapes=[
            pltpu.VMEM((SECTORS, 2, STATES, STATES), F32),
            pltpu.VMEM((SECTORS, 2 * STATES, 3 * STATES), BF16),
            pltpu.VMEM((PAIRS, STATES, STATES), F32),
            pltpu.VMEM((PAIRS, STATES, STATES), F32),
            pltpu.VMEM((2, 2, 8, PAIRS, 8, 128), F32),
            pltpu.VMEM((2, 2, 8, PAIRS, 8, 128), F32),
            pltpu.VMEM((2, 2, TARGETS * 8, 128), F32),
            pltpu.VMEM((2, 2, 3, 512, 128), F32),
            pltpu.VMEM((2, 2, NZ, SECTORS * 8, 128), F32),
            pltpu.VMEM((2, 2, NZ, SECTORS * 8, 128), F32),
            pltpu.VMEM((2, 8, 8, 128), jnp.int32),
            pltpu.VMEM((2, TARGETS, 512), BF16),
            dma((3, GROUPS)), dma((2, 8)), dma((2, 8)), dma((2, 2, 8)), dma((2, 2, 8)), dma((2, 2)),
            dma((2, 2, 3)), dma((2, 2, 3)), dma((2, 2, NZ)), dma((2, 2, NZ)),
        ],
        compiler_params=pltpu.CompilerParams(
            collective_id=0, has_side_effects=True, vmem_limit_bytes=52 << 20),
        name="sigma",
    )(table, wavefunction, left, right)


def solution(mesh):
    placed = (
        P("sec", None, None, None),
        P("ops", "sec", None, None),
        P("ops", "sec", None, None),
        P("ops", None, None, None, None),
        P("ops", None, None, None),
    )
    return jax.shard_map(
        shards, mesh=mesh, in_specs=placed, out_specs=P("sec", None, "ops", None), check_vma=False
    )
```

```python
import functools
import jax
import jax.numpy as jnp
from jax import lax
from jax.experimental import pallas as pl
from jax.experimental.pallas import tpu as pltpu
from jax.sharding import PartitionSpec as P

MESH = pl.DeviceIdType.MESH
F32, BF16 = jnp.float32, jnp.bfloat16
STATES, SECTORS, TERMS, PAIRS = 128, 8, 8, 64
GROUPS, PER, CHUNKS = 4, 2, 4
TARGETS, NX, NY, NZ = 256, 4, 4, 8


def split(value):
    high = value.astype(BF16)
    return high, (value - high.astype(F32)).astype(BF16)


def dev(x, c, y, z):
    return (x * 2 + c, z * NY + y)


def kernel(tab_ref, psi_hbm, left_hbm, right_hbm, out_ref,
           psi, left, right, send, recv, dense, recvz, sendy, recvy, recv2, sendz, recv3,
           sendt, recvt, tabs, hot,
           in_sem, tab_s, tab_r, s1_s, s1_r, own_sem, z_s, z_r, y_s, y_r,
           s2_s, s2_r, s3_s, s3_r, t_s, t_r):
    o, s = lax.axis_index("ops"), lax.axis_index("sec")
    x, c, y, z = o // 2, o % 2, s % NY, s // NY
    own = (o, y * 2 + c)
    side = (y, x)

    def row_peer(v, r):
        return dev(r // 2, r % 2, y, z) if v == 0 else dev(x, r % 2, r // 2, z)

    def side_peer(v, b):
        return dev(x, c, b, z) if v == 0 else dev(b, c, y, z)

    def far_peer(b):
        return dev(x, c, y, b)

    flipped = dev(y, c, x, z)

    psi_copy = pltpu.make_async_copy(psi_hbm, psi, in_sem.at[2, 0])
    psi_copy.start()

    def block_copies(j):
        return (
            pltpu.make_async_copy(left_hbm.at[:, j], left.at[j], in_sem.at[0, j]),
            pltpu.make_async_copy(right_hbm.at[:, j], right.at[j], in_sem.at[1, j]),
        )

    for j in range(SECTORS):
        for copy in block_copies(j):
            copy.start()

    barrier = pltpu.get_barrier_semaphore()

    def greet(peer):
        pl.semaphore_signal(barrier, inc=1, device_id=peer, device_id_type=MESH)

    def other(v, d):
        return (own[v] // 2 + d // 2) % 4 * 2 + (c + d) % 2

    for d in range(1, 8):
        greet(row_peer(0, other(0, d)))
        if d != 1:
            greet(row_peer(1, other(1, d)))
        greet(far_peer((z + d) % NZ))

    @pl.when(x != y)
    def _():
        greet(flipped)

    pl.semaphore_wait(barrier, jnp.where(x == y, 20, 21))

    def remote(src, dst, ssem, rsem, peer):
        return pltpu.make_async_remote_copy(
            src_ref=src, dst_ref=dst, send_sem=ssem, recv_sem=rsem,
            device_id=peer, device_id_type=MESH)

    def tab_copy(v, d, slot):
        r = other(v, d)
        return remote(tab_ref, tabs.at[v, slot], tab_s.at[v, r], tab_r.at[v, slot], row_peer(v, r))

    def row_copy(v, q, d, part):
        r = other(v, d)
        return remote(send.at[v, q, r, part], recv.at[v, q, own[v], part],
                      s1_s.at[v, q, r], s1_r.at[v, q, own[v]], row_peer(v, r))

    def row_wait(v, q, d):
        r = other(v, d)
        return remote(send.at[v, q, r], recv.at[v, q, r],
                      s1_s.at[v, q, r], s1_r.at[v, q, r], row_peer(v, r))

    def own_copy(v, q):
        return pltpu.make_async_copy(send.at[v, q, own[v]], recv.at[v, q, own[v]], own_sem.at[v, q])

    def z_copy(v, q, d):
        b = (z + d) % NZ
        return remote(dense.at[v, q, :, b], recvz.at[v, q, d],
                      z_s.at[v, q, d], z_r.at[v, q, d], far_peer(b))

    def y_copy(v, q, d):
        b = (side[v] + d) % 4
        return remote(sendy.at[v, q, b], recvy.at[v, q, d],
                      y_s.at[v, q, d], y_r.at[v, q, d], side_peer(v, b))

    def s2_copy(v, q, d):
        b = (side[v] + d) % 4
        return remote(dense.at[v, q, b], recv2.at[v, q - 2, d],
                      s2_s.at[v, q - 2, d], s2_r.at[v, q - 2, d], side_peer(v, b))

    def s3_copy(v, q, d):
        b = (z + d) % NZ
        return remote(sendz.at[v, q - 2, b], recv3.at[v, q - 2, d],
                      s3_s.at[v, q - 2, d], s3_r.at[v, q - 2, d], far_peer(b))

    def flip_copy(q):
        return remote(sendt.at[q], recvt.at[q], t_s.at[q], t_r.at[q], flipped)

    for d in range(1, 8):
        for v in range(2):
            tab_copy(v, d, own[v]).start()
    for v in range(2):
        tabs[v, own[v]] = tab_ref[...]

    psi_copy.wait()

    @pl.loop(0, GROUPS)
    def _(g):
        for i in range(PER):
            j = g * PER + i
            for copy in block_copies(j):
                copy.wait()
            high, low = split(psi[j].reshape(2 * STATES, STATES))
            vectors = jnp.concatenate([high, high, low], axis=1)
            high, low = split(right[j].reshape(TERMS * STATES, STATES))
            halves = lax.dot_general(
                jnp.concatenate([high, low, high], axis=1), vectors,
                (((1,), (1,)), ((), ())), preferred_element_type=F32)
            for k in range(TERMS):
                half = halves[STATES * k:STATES * (k + 1)]
                high, low = split(jnp.concatenate([half[:, :STATES], half[:, STATES:]], axis=0))
                operand = jnp.concatenate([high, low, high], axis=1)
                high, low = split(left[j, k])
                product = lax.dot_general(
                    jnp.concatenate([high, high, low], axis=1), operand,
                    (((1,), (1,)), ((), ())), preferred_element_type=F32)
                for t in range(32):
                    for v in range(2):
                        send[v, t % CHUNKS, t // CHUNKS, j, 4 * k:4 * k + 4, :] = product[
                            4 * t:4 * t + 4, STATES * v:STATES * (v + 1)]

        for d in range(1, 8):
            for v in range(2):
                row_copy(v, 0, d, pl.ds(g * PER, PER)).start()

    def start_rows(q):
        for d in range(1, 8):
            for v in range(2):
                row_copy(v, q, d, pl.ds(0, SECTORS)).start()

    start_rows(1)
    for q in range(CHUNKS):
        for v in range(2):
            own_copy(v, q).start()

    for v in range(2):
        for d in range(1, 8):
            tab_copy(v, d, other(v, d)).wait()
        for e in range(4):
            line = tabs[v, 2 * e][0:1, :] + tabs[v, 2 * e + 1][0:1, :]
            number = lax.broadcasted_iota(jnp.int32, (TARGETS, 128), 0)
            hot[v, :, 128 * e:128 * (e + 1)] = (number == line).astype(F32).astype(BF16)

    def sum_rows(q):
        for v in range(2):
            for d in range(1, 8):
                row_wait(v, q, d).wait_recv()
            own_copy(v, q).wait()
        if q + 2 < CHUNKS:
            start_rows(q + 2)
        for v in range(2):
            flat = recv.at[v, q].reshape(8 * PAIRS * 4, 128)
            sums = dense.at[v, q].reshape(TARGETS * 4, 128)
            for i in range(4):
                high, low = split(flat[pl.ds(i, 8 * PAIRS, stride=4), :])
                total = jnp.dot(hot[v], jnp.concatenate([high, low], axis=1), preferred_element_type=F32)
                sums[pl.ds(i, TARGETS, stride=4), :] = total[:, :128] + total[:, 128:]
            if q < 2:
                for d in range(1, NZ):
                    z_copy(v, q, d).start()
            else:
                for d in range(1, 4):
                    s2_copy(v, q, d).start()

    def finish(v, q, total):
        if v == 0:
            for n in range(SECTORS):
                out_ref[n, 0, 4 * q:4 * q + 4, :] = total[4 * n:4 * n + 4]
        else:
            sendt[q] = total

            @pl.when(x != y)
            def _():
                flip_copy(q).start()

            @pl.when(x == y)
            def _():
                recvt[q] = total

    def z_middle(q):
        for v in range(2):
            for d in range(1, NZ):
                z_copy(v, q, d).wait_recv()
            total = dense[v, q, :, z]
            for d in range(1, NZ):
                total = total + recvz[v, q, d]
            sendy[v, q] = total
            for d in range(1, 4):
                y_copy(v, q, d).start()

    def z_last(q):
        for v in range(2):
            for d in range(1, 4):
                y_copy(v, q, d).wait_recv()
            finish(v, q, sendy[v, q, side[v]] + recvy[v, q, 1] + recvy[v, q, 2] + recvy[v, q, 3])

    def s_middle(q):
        for v in range(2):
            for d in range(1, 4):
                s2_copy(v, q, d).wait_recv()
            sendz[v, q - 2] = (dense[v, q, side[v]] + recv2[v, q - 2, 1]) + (
                recv2[v, q - 2, 2] + recv2[v, q - 2, 3])
            for d in range(1, NZ):
                s3_copy(v, q, d).start()

    def s_last(q):
        for v in (1, 0):
            for d in range(1, NZ):
                s3_copy(v, q, d).wait_recv()
            total = sendz[v, q - 2, z]
            for d in range(1, NZ):
                total = total + recv3[v, q - 2, d]
            finish(v, q, total)

    sum_rows(0)
    sum_rows(1)
    sum_rows(2)
    z_middle(0)
    sum_rows(3)
    z_middle(1)
    s_middle(2)
    s_middle(3)
    z_last(0)
    z_last(1)
    s_last(2)
    s_last(3)

    for q in range(CHUNKS):
        @pl.when(x != y)
        def _():
            flip_copy(q).wait()

        for n in range(SECTORS):
            out_ref[n, 1, 4 * q:4 * q + 4, :] = recvt[q, 4 * n:4 * n + 4, :]

    for v in range(2):
        for q in range(CHUNKS):
            for d in range(1, 8):
                row_wait(v, q, d).wait_send()
        for q in range(2):
            for d in range(1, NZ):
                z_copy(v, q, d).wait_send()
                s3_copy(v, q + 2, d).wait_send()
            for d in range(1, 4):
                y_copy(v, q, d).wait_send()
                s2_copy(v, q + 2, d).wait_send()


def shards(wavefunction, left_blocks, right_blocks, target_owner, target_local):
    o, s = lax.axis_index("ops"), lax.axis_index("sec")
    owner = lax.dynamic_index_in_dim(target_owner[0, :, :, :, 0], s, 0, keepdims=False)
    local = lax.dynamic_index_in_dim(target_local[0], s, 0, keepdims=False)
    number = owner % NY * (NZ * SECTORS) + owner // NY * SECTORS + local
    line = number.T.reshape(1, PAIRS)
    lanes = jnp.arange(128, dtype=jnp.int32)[None, :]
    table = jnp.where(lanes // PAIRS == o % 2, jnp.concatenate([line, line], axis=1), 0)
    table = jnp.broadcast_to(table, (8, 128))
    far = pl.BlockSpec(memory_space=pltpu.HBM)
    near = pl.BlockSpec(memory_space=pltpu.VMEM)
    dma = pltpu.SemaphoreType.DMA

    def vmem(*shape):
        return pltpu.VMEM(shape, F32)

    return pl.pallas_call(
        kernel,
        out_shape=jax.ShapeDtypeStruct((SECTORS, 2, 16, STATES), F32),
        in_specs=[near, far, far, far],
        out_specs=near,
        scratch_shapes=[
            vmem(SECTORS, 2, STATES, STATES),
            vmem(SECTORS, TERMS, STATES, STATES),
            vmem(SECTORS, TERMS, STATES, STATES),
            vmem(2, CHUNKS, 8, SECTORS, 4 * TERMS, 128),
            vmem(2, CHUNKS, 8, SECTORS, 4 * TERMS, 128),
            vmem(2, CHUNKS, 4, NZ, 4 * SECTORS, 128),
            vmem(2, 2, NZ, 4, 4 * SECTORS, 128),
            vmem(2, 2, 4, 4 * SECTORS, 128),
            vmem(2, 2, 4, 4 * SECTORS, 128),
            vmem(2, 2, 4, NZ, 4 * SECTORS, 128),
            vmem(2, 2, NZ, 4 * SECTORS, 128),
            vmem(2, 2, NZ, 4 * SECTORS, 128),
            vmem(CHUNKS, 4 * SECTORS, 128),
            vmem(CHUNKS, 4 * SECTORS, 128),
            pltpu.VMEM((2, 8, 8, 128), jnp.int32),
            pltpu.VMEM((2, TARGETS, 512), BF16),
            dma((3, SECTORS)), dma((2, 8)), dma((2, 8)),
            dma((2, CHUNKS, 8)), dma((2, CHUNKS, 8)), dma((2, CHUNKS)),
            dma((2, 2, NZ)), dma((2, 2, NZ)), dma((2, 2, 4)), dma((2, 2, 4)),
            dma((2, 2, 4)), dma((2, 2, 4)), dma((2, 2, NZ)), dma((2, 2, NZ)),
            dma((CHUNKS,)), dma((CHUNKS,)),
        ],
        compiler_params=pltpu.CompilerParams(
            collective_id=0, has_side_effects=True, vmem_limit_bytes=52 << 20),
        name="sigma",
    )(table, wavefunction, left_blocks, right_blocks)


def solution(mesh):
    placed = (
        P("sec", None, None, None),
        P("ops", "sec", None, None),
        P("ops", "sec", None, None),
        P("ops", None, None, None, None),
        P("ops", None, None, None),
    )
    return jax.shard_map(
        shards, mesh=mesh, in_specs=placed, out_specs=P("sec", None, "ops", None), check_vma=False
    )
```

```python
import functools
import jax
import jax.numpy as jnp
from jax import lax
from jax.experimental import pallas as pl
from jax.experimental.pallas import tpu as pltpu
from jax.sharding import PartitionSpec as P

MESH = pl.DeviceIdType.MESH
F32, BF16 = jnp.float32, jnp.bfloat16
STATES, SECTORS, TERMS, PAIRS = 128, 8, 8, 64
GROUPS, PER, CHUNKS = 4, 2, 4
ROWS, FIRST = (6, 6, 2, 2), (0, 8, 6, 14)
TARGETS, NX, NY, NZ = 256, 4, 4, 8


def split(value):
    high = value.astype(BF16)
    return high, (value - high.astype(F32)).astype(BF16)


def dev(x, c, y, z):
    return (x * 2 + c, z * NY + y)


def kernel(tab_ref, psi_hbm, left_hbm, right_hbm, out_ref, *scratch):
    parts = iter(scratch)

    def take(count):
        return [next(parts) for _ in range(count)]

    psi, left, right, tabs, hot = take(5)
    send, recv, dense = take(CHUNKS), take(CHUNKS), take(CHUNKS)
    chain = take(2)
    sendy, recvy = take(2), take(2)
    recv2, sendz, recv3 = take(2), take(2), take(2)
    (in_sem, tab_s, tab_r, s1_s, s1_r, own_sem, l_s, l_r,
     y_s, y_r, s2_s, s2_r, s3_s, s3_r) = take(14)
    o, s = lax.axis_index("ops"), lax.axis_index("sec")
    x, c, y, z = o // 2, o % 2, s % NY, s // NY
    own = (o, y * 2 + c)
    side = (y, x)

    def row_peer(v, r):
        return dev(r // 2, r % 2, y, z) if v == 0 else dev(x, r % 2, r // 2, z)

    def side_peer(v, b):
        return dev(x, c, b, z) if v == 0 else dev(b, c, y, z)

    def home_peer(v, b):
        return dev(x, c, y, b) if v == 0 else dev(y, c, x, b)

    psi_copy = pltpu.make_async_copy(psi_hbm, psi, in_sem.at[2, 0])
    psi_copy.start()

    def block_copies(j):
        return (
            pltpu.make_async_copy(left_hbm.at[:, j], left.at[j], in_sem.at[0, j]),
            pltpu.make_async_copy(right_hbm.at[:, j], right.at[j], in_sem.at[1, j]),
        )

    for j in range(SECTORS):
        for copy in block_copies(j):
            copy.start()

    barrier = pltpu.get_barrier_semaphore()

    def greet(peer):
        pl.semaphore_signal(barrier, inc=1, device_id=peer, device_id_type=MESH)

    def other(v, d):
        return (own[v] // 2 + d // 2) % 4 * 2 + (c + d) % 2

    for d in range(1, 8):
        greet(row_peer(0, other(0, d)))
        if d != 1:
            greet(row_peer(1, other(1, d)))
        greet(home_peer(0, (z + d) % NZ))
    for d in range(1, 4):
        greet(dev((y + d) % 4, c, x, z))

    @pl.when(x != y)
    def _():
        greet(dev(y, c, x, z))
        for d in range(NZ):
            greet(home_peer(1, (z + d) % NZ))

    def remote(src, dst, ssem, rsem, peer):
        return pltpu.make_async_remote_copy(
            src_ref=src, dst_ref=dst, send_sem=ssem, recv_sem=rsem,
            device_id=peer, device_id_type=MESH)

    def tab_copy(v, d, slot):
        r = other(v, d)
        return remote(tab_ref, tabs.at[v, slot], tab_s.at[v, r], tab_r.at[v, slot], row_peer(v, r))

    def row_copy(v, q, d, part):
        r = other(v, d)
        return remote(send[q].at[v, r, part], recv[q].at[v, own[v], part],
                      s1_s.at[v, q, r], s1_r.at[v, q, own[v]], row_peer(v, r))

    def row_wait(v, q, d):
        r = other(v, d)
        return remote(send[q].at[v, r], recv[q].at[v, r],
                      s1_s.at[v, q, r], s1_r.at[v, q, r], row_peer(v, r))

    def own_copy(v, q):
        return pltpu.make_async_copy(send[q].at[v, own[v]], recv[q].at[v, own[v]], own_sem.at[v, q])

    def hops(v, way):
        return 4 if v == way else 3

    def link_copy(v, q, way, k):
        b = (z + 1 - 2 * way) % NZ
        far = (z + (1 - 2 * way) * hops(v, way)) % NZ
        source = dense[q].at[v, :, far] if k == 1 else chain[q].at[v, way, k - 2]
        return remote(source, chain[q].at[v, way, k - 1],
                      l_s.at[q, v, way, k - 1], l_r.at[q, v, way, k - 1], home_peer(0, b))

    def link(q, k):
        for v in range(2):
            for way in range(2):
                if k > hops(v, way):
                    continue
                if k > 1:
                    link_copy(v, q, way, k - 1).wait_recv()
                    b = (z + (1 - 2 * way) * (hops(v, way) - k + 1)) % NZ
                    chain[q][v, way, k - 2] = chain[q][v, way, k - 2] + dense[q][v, :, b]
                link_copy(v, q, way, k).start()

    def y_copy(v, q, d):
        b = (side[0] + d) % 4
        if v == 0:
            return remote(sendy[q].at[0, b], recvy[q].at[0, d],
                          y_s.at[q, 0, d], y_r.at[q, 0, d], dev(x, c, b, z))
        return remote(sendy[q].at[1, b], recvy[q].at[1, x],
                      y_s.at[q, 1, d], y_r.at[q, 1, x], dev(y, c, b, z))

    def y_wait(v, q, d):
        if v == 0:
            return y_copy(v, q, d)
        a = (y + d) % 4
        return remote(sendy[q].at[1, a], recvy[q].at[1, a],
                      y_s.at[q, 1, d], y_r.at[q, 1, a], dev(a, c, x, z))

    def s2_copy(v, q, d):
        b = (side[v] + d) % 4
        return remote(dense[q].at[v, b], recv2[q - 2].at[v, d],
                      s2_s.at[q - 2, v, d], s2_r.at[q - 2, v, d], side_peer(v, b))

    def s3_copy(v, q, d):
        b = (z + d) % NZ
        return remote(sendz[q - 2].at[v, b], recv3[q - 2].at[v, d],
                      s3_s.at[q - 2, v, d], s3_r.at[q - 2, v, d], home_peer(v, b))

    def compute(g):
        for i in range(PER):
            j = g * PER + i
            for copy in block_copies(j):
                copy.wait()
            high, low = split(psi[j].reshape(2 * STATES, STATES))
            vectors = jnp.concatenate([high, high, low], axis=1)
            high, low = split(right[j].reshape(TERMS * STATES, STATES))
            halves = lax.dot_general(
                jnp.concatenate([high, low, high], axis=1), vectors,
                (((1,), (1,)), ((), ())), preferred_element_type=F32)
            for k in range(TERMS):
                half = halves[STATES * k:STATES * (k + 1)]
                high, low = split(jnp.concatenate([half[:, :STATES], half[:, STATES:]], axis=0))
                operand = jnp.concatenate([high, low, high], axis=1)
                high, low = split(left[j, k])
                product = lax.dot_general(
                    jnp.concatenate([high, high, low], axis=1), operand,
                    (((1,), (1,)), ((), ())), preferred_element_type=F32)
                for r in range(8):
                    for q in range(CHUNKS):
                        n = ROWS[q]
                        first = 16 * r + FIRST[q]
                        for v in range(2):
                            send[q][v, r, j, n * k:n * k + n, :] = product[
                                first:first + n, STATES * v:STATES * (v + 1)]

    def start_group(g):
        for d in range(1, 8):
            for v in range(2):
                row_copy(v, 0, d, pl.ds(g * PER, PER)).start()

    psi_copy.wait()
    compute(0)
    pl.semaphore_wait(barrier, jnp.where(x == y, 23, 32))
    start_group(0)
    for d in range(1, 8):
        for v in range(2):
            tab_copy(v, d, own[v]).start()
    for v in range(2):
        tabs[v, own[v]] = tab_ref[...]

    @pl.loop(1, GROUPS)
    def _(g):
        compute(g)
        start_group(g)

    def start_rows(q):
        for d in range(1, 8):
            for v in range(2):
                row_copy(v, q, d, pl.ds(0, SECTORS)).start()

    start_rows(1)
    for q in range(CHUNKS):
        for v in range(2):
            own_copy(v, q).start()

    for v in range(2):
        for d in range(1, 8):
            tab_copy(v, d, other(v, d)).wait()
        for e in range(4):
            line = tabs[v, 2 * e][0:1, :] + tabs[v, 2 * e + 1][0:1, :]
            number = lax.broadcasted_iota(jnp.int32, (TARGETS, 128), 0)
            hot[v, :, 128 * e:128 * (e + 1)] = (number == line).astype(F32).astype(BF16)

    def sum_rows(q):
        n = ROWS[q]
        for v in range(2):
            for d in range(1, 8):
                row_wait(v, q, d).wait_recv()
            own_copy(v, q).wait()
        if q + 2 < CHUNKS:
            start_rows(q + 2)
        for v in range(2):
            flat = recv[q].at[v].reshape(8 * PAIRS * n, 128)
            sums = dense[q].at[v].reshape(TARGETS * n, 128)
            for i in range(n):
                high, low = split(flat[pl.ds(i, 8 * PAIRS, stride=n), :])
                total = jnp.dot(hot[v], jnp.concatenate([high, low], axis=1), preferred_element_type=F32)
                sums[pl.ds(i, TARGETS, stride=n), :] = total[:, :128] + total[:, 128:]
            if q >= 2:
                for d in range(1, 4):
                    s2_copy(v, q, d).start()
        if q < 2:
            link(q, 1)

    def finish(v, q, total):
        n = ROWS[q]
        for i in range(SECTORS):
            out_ref[i, v, FIRST[q]:FIRST[q] + n, :] = total[n * i:n * i + n]

    def start_y(v, q):
        for d in range(1, 4):
            y_copy(v, q, d).start()
        if v == 1:
            @pl.when(x != y)
            def _():
                y_copy(1, q, 0).start()

            @pl.when(x == y)
            def _():
                recvy[q][1, x] = sendy[q][1, x]

    def middle(q):
        for v in (1, 0):
            for way in range(2):
                link_copy(v, q, way, hops(v, way)).wait_recv()
            sendy[q][v] = dense[q][v, :, z] + (
                chain[q][v, 0, hops(v, 0) - 1] + chain[q][v, 1, hops(v, 1) - 1])
            start_y(v, q)

    def last_y(q):
        for v in range(2):
            for d in range(1, 4):
                y_wait(v, q, d).wait_recv()
            if v == 1:
                @pl.when(x != y)
                def _():
                    y_wait(1, q, 0).wait_recv()
            first = sendy[q][0, y] if v == 0 else recvy[q][1, 0]
            finish(v, q, (first + recvy[q][v, 1]) + (recvy[q][v, 2] + recvy[q][v, 3]))

    def s_middle(q):
        for v in (1, 0):
            for d in range(1, 4):
                s2_copy(v, q, d).wait_recv()
            sendz[q - 2][v] = (dense[q][v, side[v]] + recv2[q - 2][v, 1]) + (
                recv2[q - 2][v, 2] + recv2[q - 2][v, 3])
            for d in range(1, NZ):
                s3_copy(v, q, d).start()
            if v == 1:
                @pl.when(x != y)
                def _():
                    s3_copy(1, q, 0).start()

                @pl.when(x == y)
                def _():
                    recv3[q - 2][1, 0] = sendz[q - 2][1, z]

    def s_last(q):
        for v in range(2):
            for d in range(1, NZ):
                s3_copy(v, q, d).wait_recv()
            if v == 1:
                @pl.when(x != y)
                def _():
                    s3_copy(1, q, 0).wait_recv()
            total = sendz[q - 2][0, z] if v == 0 else recv3[q - 2][1, 0]
            for d in range(1, NZ):
                total = total + recv3[q - 2][v, d]
            finish(v, q, total)

    sum_rows(0)
    link(0, 2)
    link(0, 3)
    sum_rows(1)
    link(0, 4)
    link(1, 2)
    middle(0)
    sum_rows(2)
    link(1, 3)
    sum_rows(3)
    s_middle(2)
    link(1, 4)
    s_middle(3)
    middle(1)
    last_y(0)
    s_last(2)
    s_last(3)
    last_y(1)

    for v in range(2):
        for q in range(CHUNKS):
            for d in range(1, 8):
                row_wait(v, q, d).wait_send()
        for q in range(2):
            for way in range(2):
                for k in range(hops(v, way)):
                    link_copy(v, q, way, k + 1).wait_send()
            for d in range(1, 4):
                y_copy(v, q, d).wait_send()
                s2_copy(v, q + 2, d).wait_send()
            for d in range(1, NZ):
                s3_copy(v, q + 2, d).wait_send()

    @pl.when(x != y)
    def _():
        for q in range(2):
            y_copy(1, q, 0).wait_send()
            s3_copy(1, q + 2, 0).wait_send()


def shards(wavefunction, left_blocks, right_blocks, target_owner, target_local):
    o, s = lax.axis_index("ops"), lax.axis_index("sec")
    owner = lax.dynamic_index_in_dim(target_owner[0, :, :, :, 0], s, 0, keepdims=False)
    local = lax.dynamic_index_in_dim(target_local[0], s, 0, keepdims=False)
    number = owner % NY * (NZ * SECTORS) + owner // NY * SECTORS + local
    line = number.T.reshape(1, PAIRS)
    lanes = jnp.arange(128, dtype=jnp.int32)[None, :]
    table = jnp.where(lanes // PAIRS == o % 2, jnp.concatenate([line, line], axis=1), 0)
    table = jnp.broadcast_to(table, (8, 128))
    far = pl.BlockSpec(memory_space=pltpu.HBM)
    near = pl.BlockSpec(memory_space=pltpu.VMEM)
    dma = pltpu.SemaphoreType.DMA

    def vmem(*shape):
        return pltpu.VMEM(shape, F32)

    return pl.pallas_call(
        kernel,
        out_shape=jax.ShapeDtypeStruct((SECTORS, 2, 16, STATES), F32),
        in_specs=[near, far, far, far],
        out_specs=near,
        scratch_shapes=[
            vmem(SECTORS, 2, STATES, STATES),
            vmem(SECTORS, TERMS, STATES, STATES),
            vmem(SECTORS, TERMS, STATES, STATES),
            pltpu.VMEM((2, 8, 8, 128), jnp.int32),
            pltpu.VMEM((2, TARGETS, 512), BF16),
            *[vmem(2, 8, SECTORS, n * TERMS, 128) for n in ROWS],
            *[vmem(2, 8, SECTORS, n * TERMS, 128) for n in ROWS],
            *[vmem(2, 4, NZ, n * SECTORS, 128) for n in ROWS],
            *[vmem(2, 2, 4, 4, n * SECTORS, 128) for n in ROWS[:2]],
            *[vmem(2, 4, n * SECTORS, 128) for n in ROWS[:2]],
            *[vmem(2, 4, n * SECTORS, 128) for n in ROWS[:2]],
            *[vmem(2, 4, NZ, n * SECTORS, 128) for n in ROWS[2:]],
            *[vmem(2, NZ, n * SECTORS, 128) for n in ROWS[2:]],
            *[vmem(2, NZ, n * SECTORS, 128) for n in ROWS[2:]],
            dma((3, SECTORS)), dma((2, 8)), dma((2, 8)),
            dma((2, CHUNKS, 8)), dma((2, CHUNKS, 8)), dma((2, CHUNKS)),
            dma((2, 2, 2, 4)), dma((2, 2, 2, 4)),
            dma((2, 2, 4)), dma((2, 2, 4)), dma((2, 2, 4)), dma((2, 2, 4)),
            dma((2, 2, NZ)), dma((2, 2, NZ)),
        ],
        compiler_params=pltpu.CompilerParams(
            collective_id=0, has_side_effects=True, vmem_limit_bytes=62 << 20),
        name="sigma",
    )(table, wavefunction, left_blocks, right_blocks)


def solution(mesh):
    placed = (
        P("sec", None, None, None),
        P("ops", "sec", None, None),
        P("ops", "sec", None, None),
        P("ops", None, None, None, None),
        P("ops", None, None, None),
    )
    return jax.shard_map(
        shards, mesh=mesh, in_specs=placed, out_specs=P("sec", None, "ops", None), check_vma=False
    )
```

```python
import functools
import jax
import jax.numpy as jnp
from jax import lax
from jax.experimental import pallas as pl
from jax.experimental.pallas import tpu as pltpu
from jax.sharding import PartitionSpec as P

MESH = pl.DeviceIdType.MESH
F32, BF16 = jnp.float32, jnp.bfloat16
STATES, SECTORS, TERMS, PAIRS = 128, 8, 8, 64
GROUPS, PER, CHUNKS = 4, 2, 4
ROWS, FIRST = (6, 6, 2, 2), (0, 8, 6, 14)
TARGETS, NX, NY, NZ = 256, 4, 4, 8


def split(value):
    high = value.astype(BF16)
    return high, (value - high.astype(F32)).astype(BF16)


def dev(x, c, y, z):
    return (x * 2 + c, z * NY + y)


def kernel(tab_ref, psi_hbm, left_hbm, right_hbm, out_ref, *scratch):
    parts = iter(scratch)

    def take(count):
        return [next(parts) for _ in range(count)]

    psi, left, right, tabs, hot = take(5)
    send, recv, dense = take(CHUNKS), take(CHUNKS), take(CHUNKS)
    chain = take(2)
    sendy, recvy = take(2), take(2)
    recv2, sendz, recv3 = take(2), take(2), take(2)
    sendt, recvt = take(2)
    (in_sem, tab_s, tab_r, s1_s, s1_r, own_sem, l_s, l_r,
     y_s, y_r, s2_s, s2_r, s3_s, s3_r, t_s, t_r) = take(16)
    o, s = lax.axis_index("ops"), lax.axis_index("sec")
    x, c, y, z = o // 2, o % 2, s % NY, s // NY
    own = (o, y * 2 + c)
    side = (y, x)

    def row_peer(v, r):
        return dev(r // 2, r % 2, y, z) if v == 0 else dev(x, r % 2, r // 2, z)

    def side_peer(v, b):
        return dev(x, c, b, z) if v == 0 else dev(b, c, y, z)

    def home_peer(v, b):
        return dev(x, c, y, b) if v == 0 else dev(y, c, x, b)

    psi_copy = pltpu.make_async_copy(psi_hbm, psi, in_sem.at[2, 0])
    psi_copy.start()

    def block_copies(j):
        return (
            pltpu.make_async_copy(left_hbm.at[:, j], left.at[j], in_sem.at[0, j]),
            pltpu.make_async_copy(right_hbm.at[:, j], right.at[j], in_sem.at[1, j]),
        )

    for j in range(SECTORS):
        for copy in block_copies(j):
            copy.start()

    barrier = pltpu.get_barrier_semaphore()

    def greet(peer):
        pl.semaphore_signal(barrier, inc=1, device_id=peer, device_id_type=MESH)

    def other(v, d):
        return (own[v] // 2 + d // 2) % 4 * 2 + (c + d) % 2

    for d in range(1, 8):
        greet(row_peer(0, other(0, d)))
        if d != 1:
            greet(row_peer(1, other(1, d)))
        greet(home_peer(0, (z + d) % NZ))
    for d in range(1, 4):
        greet(dev((y + d) % 4, c, x, z))

    @pl.when(x != y)
    def _():
        greet(dev(y, c, x, z))
        for d in range(NZ):
            greet(home_peer(1, (z + d) % NZ))

    def remote(src, dst, ssem, rsem, peer):
        return pltpu.make_async_remote_copy(
            src_ref=src, dst_ref=dst, send_sem=ssem, recv_sem=rsem,
            device_id=peer, device_id_type=MESH)

    def tab_copy(v, d, slot):
        r = other(v, d)
        return remote(tab_ref, tabs.at[v, slot], tab_s.at[v, r], tab_r.at[v, slot], row_peer(v, r))

    def row_copy(v, q, d, part):
        r = other(v, d)
        return remote(send[q].at[v, r, part], recv[q].at[v, own[v], part],
                      s1_s.at[v, q, r], s1_r.at[v, q, own[v]], row_peer(v, r))

    def row_wait(v, q, d):
        r = other(v, d)
        return remote(send[q].at[v, r], recv[q].at[v, r],
                      s1_s.at[v, q, r], s1_r.at[v, q, r], row_peer(v, r))

    def own_copy(v, q):
        return pltpu.make_async_copy(send[q].at[v, own[v]], recv[q].at[v, own[v]], own_sem.at[v, q])

    def hops(v, way):
        return 4 if v == way else 3

    def link_copy(v, q, way, k):
        b = (z + 1 - 2 * way) % NZ
        far = (z + (1 - 2 * way) * hops(v, way)) % NZ
        source = dense[q].at[v, :, far] if k == 1 else chain[q].at[v, way, k - 2]
        return remote(source, chain[q].at[v, way, k - 1],
                      l_s.at[q, v, way, k - 1], l_r.at[q, v, way, k - 1], home_peer(0, b))

    def link(q, k):
        for v in range(2):
            for way in range(2):
                if k > hops(v, way):
                    continue
                if k > 1:
                    link_copy(v, q, way, k - 1).wait_recv()
                    b = (z + (1 - 2 * way) * (hops(v, way) - k + 1)) % NZ
                    chain[q][v, way, k - 2] = chain[q][v, way, k - 2] + dense[q][v, :, b]
                link_copy(v, q, way, k).start()

    def y_copy(v, q, d):
        b = (side[0] + d) % 4
        if v == 0:
            return remote(sendy[q].at[0, b], recvy[q].at[0, d],
                          y_s.at[q, 0, d], y_r.at[q, 0, d], dev(x, c, b, z))
        return remote(sendy[q].at[1, b], recvy[q].at[1, x],
                      y_s.at[q, 1, d], y_r.at[q, 1, x], dev(y, c, b, z))

    def y_wait(v, q, d):
        if v == 0:
            return y_copy(v, q, d)
        a = (y + d) % 4
        return remote(sendy[q].at[1, a], recvy[q].at[1, a],
                      y_s.at[q, 1, d], y_r.at[q, 1, a], dev(a, c, x, z))

    def s2_copy(v, q, d):
        b = (side[v] + d) % 4
        return remote(dense[q].at[v, b], recv2[q - 2].at[v, d],
                      s2_s.at[q - 2, v, d], s2_r.at[q - 2, v, d], side_peer(v, b))

    def s3_copy(v, q, d):
        b = (z + d) % NZ
        return remote(sendz[q - 2].at[v, b], recv3[q - 2].at[v, d],
                      s3_s.at[q - 2, v, d], s3_r.at[q - 2, v, d], home_peer(v * (q - 2), b))

    def flip_copy():
        return remote(sendt, recvt, t_s, t_r, dev(y, c, x, z))

    def compute(g):
        for i in range(PER):
            j = g * PER + i
            for copy in block_copies(j):
                copy.wait()
            high, low = split(psi[j].reshape(2 * STATES, STATES))
            vectors = jnp.concatenate([high, high, low], axis=1)
            high, low = split(right[j].reshape(TERMS * STATES, STATES))
            halves = lax.dot_general(
                jnp.concatenate([high, low, high], axis=1), vectors,
                (((1,), (1,)), ((), ())), preferred_element_type=F32)
            for k in range(TERMS):
                half = halves[STATES * k:STATES * (k + 1)]
                high, low = split(jnp.concatenate([half[:, :STATES], half[:, STATES:]], axis=0))
                operand = jnp.concatenate([high, low, high], axis=1)
                high, low = split(left[j, k])
                product = lax.dot_general(
                    jnp.concatenate([high, high, low], axis=1), operand,
                    (((1,), (1,)), ((), ())), preferred_element_type=F32)
                for r in range(8):
                    for q in range(CHUNKS):
                        n = ROWS[q]
                        first = 16 * r + FIRST[q]
                        for v in range(2):
                            send[q][v, r, j, n * k:n * k + n, :] = product[
                                first:first + n, STATES * v:STATES * (v + 1)]

    def start_group(g):
        for d in range(1, 8):
            for v in range(2):
                row_copy(v, 0, d, pl.ds(g * PER, PER)).start()

    psi_copy.wait()
    compute(0)
    pl.semaphore_wait(barrier, jnp.where(x == y, 23, 32))
    start_group(0)
    for d in range(1, 8):
        for v in range(2):
            tab_copy(v, d, own[v]).start()
    for v in range(2):
        tabs[v, own[v]] = tab_ref[...]

    @pl.loop(1, GROUPS)
    def _(g):
        compute(g)
        start_group(g)

    def start_rows(q):
        for d in range(1, 8):
            for v in range(2):
                row_copy(v, q, d, pl.ds(0, SECTORS)).start()

    start_rows(1)
    for q in range(CHUNKS):
        for v in range(2):
            own_copy(v, q).start()

    for v in range(2):
        for d in range(1, 8):
            tab_copy(v, d, other(v, d)).wait()
        for e in range(4):
            line = tabs[v, 2 * e][0:1, :] + tabs[v, 2 * e + 1][0:1, :]
            number = lax.broadcasted_iota(jnp.int32, (TARGETS, 128), 0)
            hot[v, :, 128 * e:128 * (e + 1)] = (number == line).astype(F32).astype(BF16)

    def sum_rows(q):
        n = ROWS[q]
        for v in range(2):
            for d in range(1, 8):
                row_wait(v, q, d).wait_recv()
            own_copy(v, q).wait()
        if q + 2 < CHUNKS:
            start_rows(q + 2)
        for v in range(2):
            flat = recv[q].at[v].reshape(8 * PAIRS * n, 128)
            sums = dense[q].at[v].reshape(TARGETS * n, 128)
            for i in range(n):
                high, low = split(flat[pl.ds(i, 8 * PAIRS, stride=n), :])
                total = jnp.dot(hot[v], jnp.concatenate([high, low], axis=1), preferred_element_type=F32)
                sums[pl.ds(i, TARGETS, stride=n), :] = total[:, :128] + total[:, 128:]
            if q >= 2:
                for d in range(1, 4):
                    s2_copy(v, q, d).start()
        if q < 2:
            link(q, 1)

    def finish(v, q, total):
        n = ROWS[q]
        for i in range(SECTORS):
            out_ref[i, v, FIRST[q]:FIRST[q] + n, :] = total[n * i:n * i + n]

    def start_y(v, q):
        for d in range(1, 4):
            y_copy(v, q, d).start()
        if v == 1:
            @pl.when(x != y)
            def _():
                y_copy(1, q, 0).start()

            @pl.when(x == y)
            def _():
                recvy[q][1, x] = sendy[q][1, x]

    def middle(q):
        for v in (1, 0):
            for way in range(2):
                link_copy(v, q, way, hops(v, way)).wait_recv()
            sendy[q][v] = dense[q][v, :, z] + (
                chain[q][v, 0, hops(v, 0) - 1] + chain[q][v, 1, hops(v, 1) - 1])
            start_y(v, q)

    def last_y(q):
        for v in range(2):
            for d in range(1, 4):
                y_wait(v, q, d).wait_recv()
            if v == 1:
                @pl.when(x != y)
                def _():
                    y_wait(1, q, 0).wait_recv()
            first = sendy[q][0, y] if v == 0 else recvy[q][1, 0]
            finish(v, q, (first + recvy[q][v, 1]) + (recvy[q][v, 2] + recvy[q][v, 3]))

    def s_middle(q):
        for v in (1, 0):
            for d in range(1, 4):
                s2_copy(v, q, d).wait_recv()
            sendz[q - 2][v] = (dense[q][v, side[v]] + recv2[q - 2][v, 1]) + (
                recv2[q - 2][v, 2] + recv2[q - 2][v, 3])
            for d in range(1, NZ):
                s3_copy(v, q, d).start()
            if v == 1 and q == 3:
                @pl.when(x != y)
                def _():
                    s3_copy(1, q, 0).start()

                @pl.when(x == y)
                def _():
                    recv3[q - 2][1, 0] = sendz[q - 2][1, z]

    def s_last(q):
        for v in (1, 0):
            for d in range(1, NZ):
                s3_copy(v, q, d).wait_recv()
            straight = v == 0 or q == 2
            if not straight:
                @pl.when(x != y)
                def _():
                    s3_copy(1, q, 0).wait_recv()
            total = sendz[q - 2][v, z] if straight else recv3[q - 2][1, 0]
            for d in range(1, NZ):
                total = total + recv3[q - 2][v, d]
            if v == 0 or q == 3:
                finish(v, q, total)
            else:
                sendt[...] = total

                @pl.when(x != y)
                def _():
                    flip_copy().start()

                @pl.when(x == y)
                def _():
                    recvt[...] = total

    def flip_last():
        @pl.when(x != y)
        def _():
            flip_copy().wait_recv()

        finish(1, 2, recvt[...])

    sum_rows(0)
    link(0, 2)
    link(0, 3)
    sum_rows(1)
    link(0, 4)
    link(1, 2)
    middle(0)
    sum_rows(2)
    link(1, 3)
    sum_rows(3)
    s_middle(2)
    link(1, 4)
    s_middle(3)
    middle(1)
    last_y(0)
    s_last(2)
    s_last(3)
    last_y(1)
    flip_last()

    for v in range(2):
        for q in range(CHUNKS):
            for d in range(1, 8):
                row_wait(v, q, d).wait_send()
        for q in range(2):
            for way in range(2):
                for k in range(hops(v, way)):
                    link_copy(v, q, way, k + 1).wait_send()
            for d in range(1, 4):
                y_copy(v, q, d).wait_send()
                s2_copy(v, q + 2, d).wait_send()
            for d in range(1, NZ):
                s3_copy(v, q + 2, d).wait_send()

    @pl.when(x != y)
    def _():
        for q in range(2):
            y_copy(1, q, 0).wait_send()
        s3_copy(1, 3, 0).wait_send()
        flip_copy().wait_send()


def shards(wavefunction, left_blocks, right_blocks, target_owner, target_local):
    o, s = lax.axis_index("ops"), lax.axis_index("sec")
    owner = lax.dynamic_index_in_dim(target_owner[0, :, :, :, 0], s, 0, keepdims=False)
    local = lax.dynamic_index_in_dim(target_local[0], s, 0, keepdims=False)
    number = owner % NY * (NZ * SECTORS) + owner // NY * SECTORS + local
    line = number.T.reshape(1, PAIRS)
    lanes = jnp.arange(128, dtype=jnp.int32)[None, :]
    table = jnp.where(lanes // PAIRS == o % 2, jnp.concatenate([line, line], axis=1), 0)
    table = jnp.broadcast_to(table, (8, 128))
    far = pl.BlockSpec(memory_space=pltpu.HBM)
    near = pl.BlockSpec(memory_space=pltpu.VMEM)
    dma = pltpu.SemaphoreType.DMA

    def vmem(*shape):
        return pltpu.VMEM(shape, F32)

    return pl.pallas_call(
        kernel,
        out_shape=jax.ShapeDtypeStruct((SECTORS, 2, 16, STATES), F32),
        in_specs=[near, far, far, far],
        out_specs=near,
        scratch_shapes=[
            vmem(SECTORS, 2, STATES, STATES),
            vmem(SECTORS, TERMS, STATES, STATES),
            vmem(SECTORS, TERMS, STATES, STATES),
            pltpu.VMEM((2, 8, 8, 128), jnp.int32),
            pltpu.VMEM((2, TARGETS, 512), BF16),
            *[vmem(2, 8, SECTORS, n * TERMS, 128) for n in ROWS],
            *[vmem(2, 8, SECTORS, n * TERMS, 128) for n in ROWS],
            *[vmem(2, 4, NZ, n * SECTORS, 128) for n in ROWS],
            *[vmem(2, 2, 4, 4, n * SECTORS, 128) for n in ROWS[:2]],
            *[vmem(2, 4, n * SECTORS, 128) for n in ROWS[:2]],
            *[vmem(2, 4, n * SECTORS, 128) for n in ROWS[:2]],
            *[vmem(2, 4, NZ, n * SECTORS, 128) for n in ROWS[2:]],
            *[vmem(2, NZ, n * SECTORS, 128) for n in ROWS[2:]],
            *[vmem(2, NZ, n * SECTORS, 128) for n in ROWS[2:]],
            vmem(ROWS[2] * SECTORS, 128),
            vmem(ROWS[2] * SECTORS, 128),
            dma((3, SECTORS)), dma((2, 8)), dma((2, 8)),
            dma((2, CHUNKS, 8)), dma((2, CHUNKS, 8)), dma((2, CHUNKS)),
            dma((2, 2, 2, 4)), dma((2, 2, 2, 4)),
            dma((2, 2, 4)), dma((2, 2, 4)), dma((2, 2, 4)), dma((2, 2, 4)),
            dma((2, 2, NZ)), dma((2, 2, NZ)), dma, dma,
        ],
        compiler_params=pltpu.CompilerParams(
            collective_id=0, has_side_effects=True, vmem_limit_bytes=62 << 20),
        name="sigma",
    )(table, wavefunction, left_blocks, right_blocks)


def solution(mesh):
    placed = (
        P("sec", None, None, None),
        P("ops", "sec", None, None),
        P("ops", "sec", None, None),
        P("ops", None, None, None, None),
        P("ops", None, None, None),
    )
    return jax.shard_map(
        shards, mesh=mesh, in_specs=placed, out_specs=P("sec", None, "ops", None), check_vma=False
    )
```

```python
import functools
import jax
import jax.numpy as jnp
from jax import lax
from jax.experimental import pallas as pl
from jax.experimental.pallas import tpu as pltpu
from jax.sharding import PartitionSpec as P

MESH = pl.DeviceIdType.MESH
F32, BF16 = jnp.float32, jnp.bfloat16
STATES, SECTORS, TERMS, PAIRS = 128, 8, 8, 64
GROUPS, PER, CHUNKS = 4, 2, 4
ROWS, FIRST = (6, 6, 2, 2), (0, 8, 6, 14)
TARGETS, NX, NY, NZ = 256, 4, 4, 8


def split(value):
    high = value.astype(BF16)
    return high, (value - high.astype(F32)).astype(BF16)


def dev(x, c, y, z):
    return (x * 2 + c, z * NY + y)


def kernel(tab_ref, psi_hbm, left_hbm, right_hbm, out_ref, *scratch):
    parts = iter(scratch)

    def take(count):
        return [next(parts) for _ in range(count)]

    psi, left, right, tabs, hot = take(5)
    send, recv, dense = take(CHUNKS), take(CHUNKS), take(CHUNKS)
    chain = take(2)
    sendy, recvy = take(2), take(2)
    recv2, sendz, recv3 = take(2), take(2), take(2)
    sendt, recvt = take(2)
    (in_sem, tab_s, tab_r, s1_s, s1_r, own_sem, l_s, l_r,
     y_s, y_r, s2_s, s2_r, s3_s, s3_r, t_s, t_r) = take(16)
    o, s = lax.axis_index("ops"), lax.axis_index("sec")
    x, c, y, z = o // 2, o % 2, s % NY, s // NY
    own = (o, y * 2 + c)
    side = (y, x)

    def row_peer(v, r):
        return dev(r // 2, r % 2, y, z) if v == 0 else dev(x, r % 2, r // 2, z)

    def side_peer(v, b):
        return dev(x, c, b, z) if v == 0 else dev(b, c, y, z)

    def home_peer(v, b):
        return dev(x, c, y, b) if v == 0 else dev(y, c, x, b)

    psi_copy = pltpu.make_async_copy(psi_hbm, psi, in_sem.at[2, 0])
    psi_copy.start()

    def block_copies(j):
        return (
            pltpu.make_async_copy(left_hbm.at[:, j], left.at[j], in_sem.at[0, j]),
            pltpu.make_async_copy(right_hbm.at[:, j], right.at[j], in_sem.at[1, j]),
        )

    for j in range(SECTORS):
        for copy in block_copies(j):
            copy.start()

    barrier = pltpu.get_barrier_semaphore()

    def greet(peer):
        pl.semaphore_signal(barrier, inc=1, device_id=peer, device_id_type=MESH)

    def other(v, d):
        return (own[v] // 2 + d // 2) % 4 * 2 + (c + d) % 2

    for d in range(1, 8):
        greet(row_peer(0, other(0, d)))
        if d != 1:
            greet(row_peer(1, other(1, d)))
        greet(home_peer(0, (z + d) % NZ))
    for d in range(1, 4):
        greet(dev((y + d) % 4, c, x, z))

    @pl.when(x != y)
    def _():
        greet(dev(y, c, x, z))
        for d in range(NZ):
            greet(home_peer(1, (z + d) % NZ))

    def remote(src, dst, ssem, rsem, peer):
        return pltpu.make_async_remote_copy(
            src_ref=src, dst_ref=dst, send_sem=ssem, recv_sem=rsem,
            device_id=peer, device_id_type=MESH)

    def tab_copy(v, d, slot):
        r = other(v, d)
        return remote(tab_ref, tabs.at[v, slot], tab_s.at[v, r], tab_r.at[v, slot], row_peer(v, r))

    def row_copy(v, q, d, part):
        r = other(v, d)
        return remote(send[q].at[v, r, part], recv[q].at[v, own[v], part],
                      s1_s.at[v, q, r], s1_r.at[v, q, own[v]], row_peer(v, r))

    def row_wait(v, q, d):
        r = other(v, d)
        return remote(send[q].at[v, r], recv[q].at[v, r],
                      s1_s.at[v, q, r], s1_r.at[v, q, r], row_peer(v, r))

    def own_copy(v, q):
        return pltpu.make_async_copy(send[q].at[v, own[v]], recv[q].at[v, own[v]], own_sem.at[v, q])

    def hops(v, way):
        return 4 if v == way else 3

    def link_copy(v, q, way, k):
        b = (z + 1 - 2 * way) % NZ
        far = (z + (1 - 2 * way) * hops(v, way)) % NZ
        source = dense[q].at[v, :, far] if k == 1 else chain[q].at[v, way, k - 2]
        return remote(source, chain[q].at[v, way, k - 1],
                      l_s.at[q, v, way, k - 1], l_r.at[q, v, way, k - 1], home_peer(0, b))

    def link(q, k):
        for v in range(2):
            for way in range(2):
                if k > hops(v, way):
                    continue
                if k > 1:
                    link_copy(v, q, way, k - 1).wait_recv()
                    b = (z + (1 - 2 * way) * (hops(v, way) - k + 1)) % NZ
                    chain[q][v, way, k - 2] = chain[q][v, way, k - 2] + dense[q][v, :, b]
                link_copy(v, q, way, k).start()

    def y_copy(v, q, d):
        b = (side[0] + d) % 4
        if v == 0:
            return remote(sendy[q].at[0, b], recvy[q].at[0, d],
                          y_s.at[q, 0, d], y_r.at[q, 0, d], dev(x, c, b, z))
        return remote(sendy[q].at[1, b], recvy[q].at[1, x],
                      y_s.at[q, 1, d], y_r.at[q, 1, x], dev(y, c, b, z))

    def y_wait(v, q, d):
        if v == 0:
            return y_copy(v, q, d)
        a = (y + d) % 4
        return remote(sendy[q].at[1, a], recvy[q].at[1, a],
                      y_s.at[q, 1, d], y_r.at[q, 1, a], dev(a, c, x, z))

    def s2_copy(v, q, d):
        b = (side[v] + d) % 4
        return remote(dense[q].at[v, b], recv2[q - 2].at[v, d],
                      s2_s.at[q - 2, v, d], s2_r.at[q - 2, v, d], side_peer(v, b))

    def s3_copy(v, q, d):
        b = (z + d) % NZ
        return remote(sendz[q - 2].at[v, b], recv3[q - 2].at[v, d],
                      s3_s.at[q - 2, v, d], s3_r.at[q - 2, v, d], home_peer(v * (q - 2), b))

    def flip_copy():
        return remote(sendt, recvt, t_s, t_r, dev(y, c, x, z))

    def compute(g):
        for i in range(PER):
            j = g * PER + i
            for copy in block_copies(j):
                copy.wait()
            high, low = split(psi[j].reshape(2 * STATES, STATES))
            vectors = jnp.concatenate([high, high, low], axis=1)
            high, low = split(right[j].reshape(TERMS * STATES, STATES))
            halves = lax.dot_general(
                jnp.concatenate([high, low, high], axis=1), vectors,
                (((1,), (1,)), ((), ())), preferred_element_type=F32)
            for k in range(TERMS):
                half = halves[STATES * k:STATES * (k + 1)]
                high, low = split(jnp.concatenate([half[:, :STATES], half[:, STATES:]], axis=0))
                operand = jnp.concatenate([high, low, high], axis=1)
                high, low = split(left[j, k])
                product = lax.dot_general(
                    jnp.concatenate([high, high, low], axis=1), operand,
                    (((1,), (1,)), ((), ())), preferred_element_type=F32)
                for r in range(8):
                    for q in range(CHUNKS):
                        n = ROWS[q]
                        first = 16 * r + FIRST[q]
                        for v in range(2):
                            send[q][v, r, j, n * k:n * k + n, :] = product[
                                first:first + n, STATES * v:STATES * (v + 1)]

    def start_group(g):
        for d in range(1, 8):
            for v in range(2):
                row_copy(v, 0, d, pl.ds(g * PER, PER)).start()

    psi_copy.wait()
    compute(0)
    pl.semaphore_wait(barrier, jnp.where(x == y, 23, 32))
    start_group(0)
    for d in range(1, 8):
        for v in range(2):
            tab_copy(v, d, own[v]).start()
    for v in range(2):
        tabs[v, own[v]] = tab_ref[...]

    @pl.loop(1, GROUPS)
    def _(g):
        compute(g)
        start_group(g)

    def start_rows(q):
        for d in range(1, 8):
            for v in range(2):
                row_copy(v, q, d, pl.ds(0, SECTORS)).start()

    start_rows(1)
    for q in range(CHUNKS):
        for v in range(2):
            own_copy(v, q).start()

    for v in range(2):
        for d in range(1, 8):
            tab_copy(v, d, other(v, d)).wait()
        for e in range(4):
            line = tabs[v, 2 * e][0:1, :] + tabs[v, 2 * e + 1][0:1, :]
            number = lax.broadcasted_iota(jnp.int32, (TARGETS, 128), 0)
            hot[v, :, 128 * e:128 * (e + 1)] = (number == line).astype(F32).astype(BF16)

    def sum_rows(q):
        n = ROWS[q]
        for v in range(2):
            for d in range(1, 8):
                row_wait(v, q, d).wait_recv()
            own_copy(v, q).wait()
        if q + 2 < CHUNKS:
            start_rows(q + 2)
        for v in range(2):
            flat = recv[q].at[v].reshape(8 * PAIRS * n, 128)
            sums = dense[q].at[v].reshape(TARGETS * n, 128)
            for i in range(n):
                high, low = split(flat[pl.ds(i, 8 * PAIRS, stride=n), :])
                total = jnp.dot(hot[v], jnp.concatenate([high, low], axis=1), preferred_element_type=F32)
                sums[pl.ds(i, TARGETS, stride=n), :] = total[:, :128] + total[:, 128:]
            if q >= 2:
                for d in range(1, 4):
                    s2_copy(v, q, d).start()
        if q < 2:
            link(q, 1)

    def finish(v, q, total):
        n = ROWS[q]
        for i in range(SECTORS):
            out_ref[i, v, FIRST[q]:FIRST[q] + n, :] = total[n * i:n * i + n]

    def start_y(v, q):
        for d in range(1, 4):
            y_copy(v, q, d).start()
        if v == 1:
            @pl.when(x != y)
            def _():
                y_copy(1, q, 0).start()

            @pl.when(x == y)
            def _():
                recvy[q][1, x] = sendy[q][1, x]

    def middle(q):
        for v in (1, 0):
            for way in range(2):
                link_copy(v, q, way, hops(v, way)).wait_recv()
            sendy[q][v] = dense[q][v, :, z] + (
                chain[q][v, 0, hops(v, 0) - 1] + chain[q][v, 1, hops(v, 1) - 1])
            start_y(v, q)

    def last_y(q):
        for v in range(2):
            for d in range(1, 4):
                y_wait(v, q, d).wait_recv()
            if v == 1:
                @pl.when(x != y)
                def _():
                    y_wait(1, q, 0).wait_recv()
            first = sendy[q][0, y] if v == 0 else recvy[q][1, 0]
            finish(v, q, (first + recvy[q][v, 1]) + (recvy[q][v, 2] + recvy[q][v, 3]))

    def s_middle(q):
        for v in (1, 0):
            for d in range(1, 4):
                s2_copy(v, q, d).wait_recv()
            sendz[q - 2][v] = (dense[q][v, side[v]] + recv2[q - 2][v, 1]) + (
                recv2[q - 2][v, 2] + recv2[q - 2][v, 3])
            for d in range(1, NZ):
                s3_copy(v, q, d).start()
            if v == 1 and q == 3:
                @pl.when(x != y)
                def _():
                    s3_copy(1, q, 0).start()

                @pl.when(x == y)
                def _():
                    recv3[q - 2][1, 0] = sendz[q - 2][1, z]

    def s_last(q):
        for v in (1, 0):
            for d in range(1, NZ):
                s3_copy(v, q, d).wait_recv()
            straight = v == 0 or q == 2
            if not straight:
                @pl.when(x != y)
                def _():
                    s3_copy(1, q, 0).wait_recv()
            total = sendz[q - 2][v, z] if straight else recv3[q - 2][1, 0]
            for d in range(1, NZ):
                total = total + recv3[q - 2][v, d]
            if v == 0 or q == 3:
                finish(v, q, total)
            else:
                sendt[...] = total

                @pl.when(x != y)
                def _():
                    flip_copy().start()

                @pl.when(x == y)
                def _():
                    recvt[...] = total

    def flip_last():
        @pl.when(x != y)
        def _():
            flip_copy().wait_recv()

        finish(1, 2, recvt[...])

    sum_rows(0)
    link(0, 2)
    link(0, 3)
    sum_rows(1)
    link(0, 4)
    link(1, 2)
    middle(0)
    sum_rows(2)
    link(1, 3)
    sum_rows(3)
    link(1, 4)
    s_middle(2)
    s_middle(3)
    middle(1)
    last_y(0)
    s_last(2)
    s_last(3)
    last_y(1)
    flip_last()

    for v in range(2):
        for q in range(CHUNKS):
            for d in range(1, 8):
                row_wait(v, q, d).wait_send()
        for q in range(2):
            for way in range(2):
                for k in range(hops(v, way)):
                    link_copy(v, q, way, k + 1).wait_send()
            for d in range(1, 4):
                y_copy(v, q, d).wait_send()
                s2_copy(v, q + 2, d).wait_send()
            for d in range(1, NZ):
                s3_copy(v, q + 2, d).wait_send()

    @pl.when(x != y)
    def _():
        for q in range(2):
            y_copy(1, q, 0).wait_send()
        s3_copy(1, 3, 0).wait_send()
        flip_copy().wait_send()


def shards(wavefunction, left_blocks, right_blocks, target_owner, target_local):
    o, s = lax.axis_index("ops"), lax.axis_index("sec")
    owner = lax.dynamic_index_in_dim(target_owner[0, :, :, :, 0], s, 0, keepdims=False)
    local = lax.dynamic_index_in_dim(target_local[0], s, 0, keepdims=False)
    number = owner % NY * (NZ * SECTORS) + owner // NY * SECTORS + local
    line = number.T.reshape(1, PAIRS)
    lanes = jnp.arange(128, dtype=jnp.int32)[None, :]
    table = jnp.where(lanes // PAIRS == o % 2, jnp.concatenate([line, line], axis=1), 0)
    table = jnp.broadcast_to(table, (8, 128))
    far = pl.BlockSpec(memory_space=pltpu.HBM)
    near = pl.BlockSpec(memory_space=pltpu.VMEM)
    dma = pltpu.SemaphoreType.DMA

    def vmem(*shape):
        return pltpu.VMEM(shape, F32)

    return pl.pallas_call(
        kernel,
        out_shape=jax.ShapeDtypeStruct((SECTORS, 2, 16, STATES), F32),
        in_specs=[near, far, far, far],
        out_specs=near,
        scratch_shapes=[
            vmem(SECTORS, 2, STATES, STATES),
            vmem(SECTORS, TERMS, STATES, STATES),
            vmem(SECTORS, TERMS, STATES, STATES),
            pltpu.VMEM((2, 8, 8, 128), jnp.int32),
            pltpu.VMEM((2, TARGETS, 512), BF16),
            *[vmem(2, 8, SECTORS, n * TERMS, 128) for n in ROWS],
            *[vmem(2, 8, SECTORS, n * TERMS, 128) for n in ROWS],
            *[vmem(2, 4, NZ, n * SECTORS, 128) for n in ROWS],
            *[vmem(2, 2, 4, 4, n * SECTORS, 128) for n in ROWS[:2]],
            *[vmem(2, 4, n * SECTORS, 128) for n in ROWS[:2]],
            *[vmem(2, 4, n * SECTORS, 128) for n in ROWS[:2]],
            *[vmem(2, 4, NZ, n * SECTORS, 128) for n in ROWS[2:]],
            *[vmem(2, NZ, n * SECTORS, 128) for n in ROWS[2:]],
            *[vmem(2, NZ, n * SECTORS, 128) for n in ROWS[2:]],
            vmem(ROWS[2] * SECTORS, 128),
            vmem(ROWS[2] * SECTORS, 128),
            dma((3, SECTORS)), dma((2, 8)), dma((2, 8)),
            dma((2, CHUNKS, 8)), dma((2, CHUNKS, 8)), dma((2, CHUNKS)),
            dma((2, 2, 2, 4)), dma((2, 2, 2, 4)),
            dma((2, 2, 4)), dma((2, 2, 4)), dma((2, 2, 4)), dma((2, 2, 4)),
            dma((2, 2, NZ)), dma((2, 2, NZ)), dma, dma,
        ],
        compiler_params=pltpu.CompilerParams(
            collective_id=0, has_side_effects=True, vmem_limit_bytes=62 << 20),
        name="sigma",
    )(table, wavefunction, left_blocks, right_blocks)


def solution(mesh):
    placed = (
        P("sec", None, None, None),
        P("ops", "sec", None, None),
        P("ops", "sec", None, None),
        P("ops", None, None, None, None),
        P("ops", None, None, None),
    )
    return jax.shard_map(
        shards, mesh=mesh, in_specs=placed, out_specs=P("sec", None, "ops", None), check_vma=False
    )
```
